32 devices in a mesh: groups: 2 (over y), wide: 4 (over z), narrow: 4 (over x, core).
Axes of the slice: x: 2, y: 2, z: 4, core: 2. Of those that a mesh axis runs over, the one named last changes fastest.
Arguments:
- target_states: bfloat16 [256, 8192], P(('groups', 'wide'), 'narrow'), parts along dimension 0, may hold values from -6 to 6
- source_states: bfloat16 [256, 8192], P(('groups', 'wide'), 'narrow'), parts along dimension 0, may hold values from -6 to 6
- target_gate: bfloat16 [8192, 14336], P('narrow', 'wide'), may hold values from -0.0625 to 0.0625
- target_up: bfloat16 [8192, 14336], P('narrow', 'wide'), may hold values from -0.0625 to 0.0625
- source_gate: bfloat16 [8192, 14336], P('narrow', 'wide'), may hold values from -0.0625 to 0.0625
- source_up: bfloat16 [8192, 14336], P('narrow', 'wide'), may hold values from -0.0625 to 0.0625
- token_ids: int32 [256], P(('groups', 'narrow')), parts along dimension 0, may hold values from 0 to 128255
- lengths: int32 [16], P(('groups', 'narrow')), parts along dimension 0, may hold values from 1 to 16
- ratio_weight: float32 [128256], replicated, may hold values from 0.25 to 1
Outputs:
- target_hidden: bfloat16 [256, 14336], P(('groups', 'narrow'), 'wide'), parts along dimension 0
- ratio_hidden: bfloat16 [256, 14336], P(('groups', 'narrow'), 'wide'), parts along dimension 0
The draws below stay inside these ranges and needn't reach their ends.
There are 2 independent parts, one for each index of `groups`. The reference program is written for one: setup_inputs(seed, part) draws one part's arguments, and reference() takes and returns one part's arrays. A program takes and returns all parts, laid end to end along the dimension named above; an argument that names none is the same for every part. Nothing has to cross between parts.
All inputs are finite; a program needn't handle non-finite values.
Results may differ from the reference program's by a relative error of at most 0.02.
Values may be sent and summed in bfloat16 or wider, within the bound.
A program may use at most 128 MiB of HBM per device.

```python
import math
import jax
import jax.numpy as jnp
import numpy as np
from jax import lax

D = 8192
FF = 14336
VOCAB = 128256
HLEN = 16
TOKENS = 128
HYPS = 8
N_NARROW = 4


def with_ends(entries, key, smallest, high):
    longest = entries.shape.index(max(entries.shape))
    spots = []
    for shift in (0, 1):
        where = [jax.random.randint(jax.random.fold_in(key, axis), (), 0, length) for axis, length in enumerate(entries.shape)]
        where[longest] = (where[longest] + shift) % entries.shape[longest]
        spots.append(tuple(where))
    return entries.at[spots[0]].set(smallest).at[spots[1]].set(high)


def block_levels(key, extent, cuts, smallest, high):
    loudness = 1.0
    for dim, parts in cuts:
        heights = jax.random.uniform(jax.random.fold_in(jax.random.fold_in(key, 6), dim), (parts,), jnp.float32, smallest / len(cuts), high / len(cuts))
        loudness = loudness * jnp.repeat(jnp.exp(heights), extent[dim] // parts).reshape((-1,) + (1,) * (len(extent) - 1 - dim))
    return loudness


def skewed_wide(own_key, extent, number_of, slope):
    loads = [min(1 << octave, number_of + 1 - (1 << octave)) * (1 << 20) // math.isqrt((1 << octave) ** slope) + 1 for octave in range((number_of + 1).bit_length()) if 1 << octave <= number_of]
    spread = 1 + sum(loads) // (1 << 30)
    listing = np.cumsum(np.array([max(1, weight // spread) for weight in loads]))
    ticket = jax.random.randint(jax.random.fold_in(own_key, 1), extent, 0, int(listing[len(loads) - 1]))
    start = jnp.left_shift(1, jnp.searchsorted(jnp.asarray(listing, jnp.int32), ticket, side="right").astype(jnp.int32))
    standing = start - 1 + jax.random.randint(jax.random.fold_in(own_key, 4), extent, 0, 1 << 30) % jnp.minimum(start, number_of + 1 - start)
    return jax.random.permutation(jax.random.fold_in(own_key, 2), number_of)[standing].astype(jnp.int32)


def scatter_about(rng, shape, deviation, reach, shards=(), held_as=jnp.bfloat16):
    array = jax.random.normal(rng, shape, jnp.float32) * deviation
    if len(shards) > 0:
        array = block_levels(rng, shape, shards, -0.22, 0.18) * array
    return jnp.clip(array, min=-reach, max=reach).astype(held_as)


def setup_inputs(seed: int = 0, part: int = 0) -> dict:
    arg_keys = jax.random.split(jax.random.key(seed), 10)
    own_keys = jax.random.split(jax.random.fold_in(arg_keys[9], part), 10)
    target_states = scatter_about(own_keys[0], (TOKENS, D), 1.0, 6.0, ((0, 4), (1, 4)))
    source_states = scatter_about(own_keys[1], (TOKENS, D), 1.0, 6.0, ((0, 4), (1, 4)))
    target_gate = scatter_about(arg_keys[2], (D, FF), D ** -0.5, 0.0625, ((0, 4), (1, 4)))
    target_up = scatter_about(arg_keys[3], (D, FF), D ** -0.5, 0.0625, ((0, 4), (1, 4)))
    source_gate = scatter_about(arg_keys[4], (D, FF), D ** -0.5, 0.0625, ((0, 4), (1, 4)))
    source_up = scatter_about(arg_keys[5], (D, FF), D ** -0.5, 0.0625, ((0, 4), (1, 4)))
    token_ids = with_ends(skewed_wide(own_keys[6], (TOKENS,), VOCAB, 2), jax.random.fold_in(own_keys[6], 3), 0, VOCAB - 1).astype(jnp.int32)
    lengths = with_ends(jax.random.randint(own_keys[7], (HYPS,), 1, HLEN + 1), jax.random.fold_in(own_keys[7], 1), 1, HLEN).astype(jnp.int32)
    ratio_weight = jnp.clip(jnp.exp(jax.random.uniform(arg_keys[8], (VOCAB,), jnp.float32, math.log(0.25), math.log(1.0))), 0.25, 1.0)
    return dict(target_states=target_states, source_states=source_states, target_gate=target_gate, target_up=target_up, source_gate=source_gate, source_up=source_up, token_ids=token_ids, lengths=lengths, ratio_weight=ratio_weight)


def projected(states, weight):
    tile = D // N_NARROW
    total = jnp.zeros((states.shape[0], weight.shape[1]), jnp.float32)
    for index in range(N_NARROW):
        partial_sum = jnp.dot(states[:, index * tile:(index + 1) * tile], weight[index * tile:(index + 1) * tile, :], preferred_element_type=jnp.float32)
        rounded = lax.optimization_barrier(partial_sum.astype(jnp.bfloat16))
        total = total + rounded.astype(jnp.float32)
    return total


def reference(target_states, source_states, target_gate, target_up, source_gate, source_up, token_ids, lengths, ratio_weight):
    target_act = jax.nn.silu(projected(target_states, target_gate)) * projected(target_states, target_up)
    source_act = jax.nn.silu(projected(source_states, source_gate)) * projected(source_states, source_up)
    slots = jnp.arange(HLEN, dtype=jnp.int32)
    live = (slots[None, :] < lengths[:, None]).reshape(-1).astype(jnp.float32)
    weight = ratio_weight[token_ids]
    target_out = (live[:, None] * target_act).astype(jnp.bfloat16)
    ratio_out = (live[:, None] * (target_act - weight[:, None] * source_act)).astype(jnp.bfloat16)
    return target_out, ratio_out
```

```python
import functools

import jax
import jax.numpy as jnp
from jax import lax
from jax.experimental import pallas as pl
from jax.experimental.pallas import tpu as pltpu
from jax.sharding import PartitionSpec as P

MESH = pl.DeviceIdType.MESH
VMEM_BYTES = 66_000_000
PIECES = (4, 2)
LAG = 2
AHEAD = (4, 3)
RELAYS = (
    (1, 2, 1, 0, 1), (3, 2, 1, 1, 1), (4, 2, 0, 0, 1), (6, 2, 0, 1, 1),
    (3, 1, 2, 0, -1), (4, 1, 2, 1, -1), (5, 1, 3, 0, -1), (6, 1, 3, 1, -1),
)


def matmul(left, right):
    return jnp.dot(left, right, preferred_element_type=jnp.float32)


def pair_project(w_gate, w_upper, piece):
    return jnp.concatenate([matmul(piece, w_gate), matmul(piece, w_upper)], axis=1)


def gated(summed, hidden_cols):
    return jax.nn.silu(summed[:, :hidden_cols]) * summed[:, hidden_cols:]


def kernel(
    tn, slots, ahead,
    ids_ref, len_ref, table_ref, ts_ref, ss_ref, tg_ref, tu_ref, sg_ref, su_ref,
    t_out, r_out,
    gath, wbuf, far_kept, near_kept, far_send, far_recv, near_send, near_recv, b_send, b_recv,
    kept, live_ref, weight_ref, table,
    table_sem, own_sem, g_send, g_recv, w_sem, fs_sem, fr_sem, ns_sem, nr_sem, bs_sem, br_sem,
):
    w = lax.axis_index("wide")
    n = lax.axis_index("narrow")
    x = n // 2
    c = n % 2
    mate = 2 * x + (1 - c)
    across = 2 * (1 - x) + c
    beside = 2 * (1 - x) + (1 - c)
    toward = 2 * x - 1
    v = x * w + (1 - x) * (3 - w)
    cols = tg_ref.shape[1]
    per = cols // tn
    units = 2 * per
    rows = gath.shape[2]
    depth = gath.shape[3]
    kept_slots = far_kept.shape[0]
    weights = ((tg_ref, tu_ref), (sg_ref, su_ref))

    def block(b):
        return x * b + (1 - x) * (3 - b)

    first = jnp.where(v == 0, block(0), block(1))
    second = jnp.where(v == 0, block(1), block(0))
    leads = across == first

    def weight_copies(u, model, j):
        span = pl.ds(pl.multiple_of(j * tn, tn), tn)
        return [
            pltpu.make_async_copy(weights[model][k].at[:, span], wbuf.at[u % slots, k], w_sem.at[u % slots, k])
            for k in range(2)
        ]

    def load(low, high):
        for u in range(low, high):
            for copy in weight_copies(u, u // per, u % per):
                copy.start()

    own = [
        pltpu.make_async_copy(ref, gath.at[m, w], own_sem.at[m])
        for m, ref in enumerate((ts_ref, ss_ref))
    ]
    for copy in own:
        copy.start()
    load(0, 2)

    barrier = pltpu.get_barrier_semaphore()

    def greet(axis, index):
        pl.semaphore_signal(barrier, inc=1, device_id={axis: index}, device_id_type=MESH)

    for gap in (-2, -1, 1, 2):
        @pl.when(jnp.logical_and(w + gap >= 0, w + gap <= 3))
        def _():
            greet("wide", w + gap)

    greet("narrow", mate)
    greet("narrow", across)
    inner = jnp.logical_and(w > 0, w < 3)
    pl.semaphore_wait(barrier, jnp.where(inner, 5, 4))

    def hop(m, b, p, step):
        size = depth // PIECES[m]
        part = gath.at[m, block(b), :, pl.ds(p * size, size)]
        way = {1: 0, -1: 1, 2: 2, -2: 2}[step]
        return pltpu.make_async_remote_copy(
            src_ref=part, dst_ref=part,
            send_sem=g_send.at[m, way, b, p], recv_sem=g_recv.at[m, b, p],
            device_id={"wide": w + toward * step}, device_id_type=MESH,
        )

    def send(m, b, *steps):
        for p in range(PIECES[m]):
            for step in steps:
                hop(m, b, p, step).start()

    def arrive(m, *blocks):
        for b in blocks:
            for p in range(PIECES[m]):
                hop(m, b, p, 1).wait_recv()

    def relay_piece(m, b, p, step):
        hop(m, b, p, 1).wait_recv()
        hop(m, b, p, step).start()

    def relay(m, b, step):
        for p in range(PIECES[m]):
            relay_piece(m, b, p, step)

    own[0].wait()

    @pl.when(v == 0)
    def _():
        send(0, 0, 1)
        send(0, 0, 2)

    @pl.when(v == 1)
    def _():
        send(0, 1, 1, -1)

    @pl.when(v == 2)
    def _():
        send(0, 2, -1, 1)

    @pl.when(v == 3)
    def _():
        send(0, 3, -1)
        send(0, 3, -2)

    own[1].wait()
    load(2, slots)
    fetch = pltpu.make_async_copy(table_ref, table, table_sem)
    fetch.start()

    @pl.when(v == 0)
    def _():
        send(1, 0, 2)
        send(1, 0, 1)

    @pl.when(v == 1)
    def _():
        relay(0, 2, -1)
        send(1, 1, 1)
        relay(0, 3, -1)
        send(1, 1, -1)

    @pl.when(v == 2)
    def _():
        relay(0, 1, 1)
        send(1, 2, -1)
        relay(0, 0, 1)

    @pl.when(v == 3)
    def _():
        send(1, 3, -2)
        send(1, 3, -1)
        arrive(0, 1)

    def relays(step):
        for at, where, b, p, way in RELAYS:
            @pl.when(jnp.logical_and(step == at, v == where))
            def _():
                relay_piece(1, b, p, way)

        @pl.when(jnp.logical_and(step == max(RELAYS)[0], v == 2))
        def _():
            send(1, 2, 1)

    def far_copy(u):
        return pltpu.make_async_remote_copy(
            src_ref=far_send.at[u], dst_ref=far_recv.at[u],
            send_sem=fs_sem.at[u], recv_sem=fr_sem.at[u],
            device_id={"narrow": mate}, device_id_type=MESH,
        )

    def near_copy(u):
        return pltpu.make_async_remote_copy(
            src_ref=near_send.at[u], dst_ref=near_recv.at[u],
            send_sem=ns_sem.at[u], recv_sem=nr_sem.at[u],
            device_id={"narrow": mate}, device_id_type=MESH,
        )

    def b_copy(u):
        return pltpu.make_async_remote_copy(
            src_ref=b_send.at[u], dst_ref=b_recv.at[u],
            send_sem=bs_sem.at[u], recv_sem=br_sem.at[u],
            device_id={"narrow": across}, device_id_type=MESH,
        )

    def cross(u):
        far_copy(u).wait_recv()
        for k in range(2):
            total = far_kept[u % kept_slots, k] + far_recv[u, k].astype(jnp.float32)
            b_send[u, k] = total.astype(jnp.bfloat16)
        b_copy(u).start()

    def tokens(model, *blocks):
        return jnp.concatenate([gath[model, i] for i in blocks], axis=0)

    def await_weights(u, model, j):
        for copy in weight_copies(u, model, j):
            copy.wait()

    def keep_far(u, k, out):
        far_kept[u % kept_slots, k] = out

    def give_far(u, k, out):
        far_send[u, k] = out.astype(jnp.bfloat16)

    def share_near(u, k, out):
        near_kept[u, k] = out[:rows]
        near_send[u, k] = out[rows:].astype(jnp.bfloat16)

    def refill(u):
        @pl.when(u + slots < units)
        def _():
            for copy in weight_copies(u + slots, 1, u + slots - per):
                copy.start()

    def phase(low, high, step0, body):
        def run(j, carry):
            relays(step0 + j - low)
            body(j)
            return carry
        lax.fori_loop(low, high, run, 0)
        return step0 + high - low

    def one_block(u, k, out, mine):
        @pl.when(mine)
        def _():
            keep_far(u, k, out)

        @pl.when(jnp.logical_not(mine))
        def _():
            give_far(u, k, out)

    def pass_on(u, mine):
        @pl.when(jnp.logical_not(mine))
        def _():
            far_copy(u).start()

        @pl.when(jnp.logical_and(mine, u >= LAG))
        def _():
            cross(u - LAG)

    def early(u):
        await_weights(u, 0, u)
        left = gath[0, first]
        for k in range(2):
            one_block(u, k, matmul(left, wbuf[u % slots, k]), leads)
        pass_on(u, leads)

    def rest(u):
        left = tokens(0, second, n, mate)
        for k in range(2):
            out = matmul(left, wbuf[u % slots, k])
            one_block(u, k, out[:rows], jnp.logical_not(leads))
            share_near(u, k, out[rows:])
        near_copy(u).start()
        pass_on(u, jnp.logical_not(leads))

        @pl.when(jnp.logical_and(leads, u < LAG))
        def _():
            cross(ahead[0] - LAG + u)

        refill(u)

    def whole(u, model):
        await_weights(u, model, u - model * per)
        left = tokens(model, across, beside, n, mate)
        for k in range(2):
            out = matmul(left, wbuf[u % slots, k])
            keep_far(u, k, out[:rows])
            give_far(u, k, out[rows:2 * rows])
            share_near(u, k, out[2 * rows:])
        far_copy(u).start()
        near_copy(u).start()

    def target(u):
        whole(u, 0)
        refill(u)

        @pl.when(jnp.logical_or(u >= ahead[0] + LAG, jnp.logical_not(leads)))
        def _():
            cross(u - LAG)

    def summed(u, k):
        near = near_kept[u, k] + near_recv[u, k].astype(jnp.float32)
        return near + b_recv[u, k].astype(jnp.float32)

    def activation(u):
        near_copy(u).wait_recv()
        b_copy(u).wait_recv()
        gate = summed(u, 0)
        return gate / (1.0 + jnp.exp(-gate)) * summed(u, 1)

    def finish_target(j):
        act = activation(j)
        kept[j] = act
        t_out[:, pl.ds(pl.multiple_of(j * tn, tn), tn)] = (live_ref[...] * act).astype(t_out.dtype)

    def finish_ratio(j, carry):
        act = activation(per + j)
        ratio = live_ref[...] * (kept[j] - weight_ref[...] * act)
        r_out[:, pl.ds(pl.multiple_of(j * tn, tn), tn)] = ratio.astype(r_out.dtype)
        return carry

    def source_far(j):
        u = per + j
        await_weights(u, 1, j)
        left = tokens(1, across, beside)
        for k in range(2):
            out = matmul(left, wbuf[u % slots, k])
            keep_far(u, k, out[:rows])
            give_far(u, k, out[rows:])
        far_copy(u).start()
        cross(u - LAG)

    def source_all(j):
        whole(per + j, 1)
        cross(per + j - LAG)
        finish_target(j - ahead[1])

    def source_near(j):
        u = per + j
        left = tokens(1, n, mate)
        for k in range(2):
            share_near(u, k, matmul(left, wbuf[u % slots, k]))
        near_copy(u).start()

        @pl.when(j < LAG)
        def _():
            cross(units - LAG + j)

        finish_target(per - ahead[1] + j)

    row = lax.broadcasted_iota(jnp.int32, (rows, 1), 0)
    hlen = rows // len_ref.shape[0]
    lived = jnp.zeros((rows, 1), jnp.float32)
    for h in range(len_ref.shape[0]):
        inside = jnp.logical_and(row >= h * hlen, row < h * hlen + len_ref[h])
        lived = jnp.where(inside, 1.0, lived)
    live_ref[...] = lived

    step = phase(0, ahead[0], 0, early)

    @pl.when(v == 0)
    def _():
        arrive(0, 1, 2, 3)

    @pl.when(v == 1)
    def _():
        arrive(0, 0)

    @pl.when(v == 2)
    def _():
        arrive(0, 3)

    @pl.when(v == 3)
    def _():
        arrive(0, 2, 0)

    step = phase(0, ahead[0], step, rest)
    step = phase(ahead[0], per, step, target)

    @pl.when(v == 0)
    def _():
        arrive(1, 1)

    @pl.when(v == 1)
    def _():
        arrive(1, 0)

    @pl.when(v == 3)
    def _():
        arrive(1, 1, 0)

    step = phase(0, ahead[1], step, source_far)

    @pl.when(v == 0)
    def _():
        arrive(1, 2, 3)

    @pl.when(v == 2)
    def _():
        arrive(1, 3)

    @pl.when(v == 3)
    def _():
        arrive(1, 2)

    step = phase(ahead[1], per, step, source_all)
    step = phase(0, ahead[1], step, source_near)

    fetch.wait()
    picked = jnp.zeros((rows, 1), jnp.float32)
    for i in range(rows):
        picked = jnp.where(row == i, table[ids_ref[i]], picked)
    weight_ref[...] = picked
    lax.fori_loop(0, per, finish_ratio, 0)

    def drain(u, carry):
        far_copy(u).wait_send()
        near_copy(u).wait_send()
        b_copy(u).wait_send()
        return carry

    lax.fori_loop(0, units, drain, 0)
    for m in range(2):
        for where, b, way in ((0, 0, 1), (0, 0, 2), (1, 1, 1), (1, 1, -1), (1, 2, -1), (1, 3, -1),
                              (2, 2, -1), (2, 2, 1), (2, 1, 1), (2, 0, 1), (3, 3, -1), (3, 3, -2)):
            @pl.when(v == where)
            def _():
                for p in range(PIECES[m]):
                    hop(m, b, p, way).wait_send()


def plan(states, weights, wide, narrow):
    depth, cols = weights.shape
    rows = states.shape[0]
    if narrow != 4 or wide != 4 or rows % 16 or depth % (128 * max(PIECES)):
        return None
    for tn in (512, 256):
        if cols % tn or cols // tn < 3:
            continue
        per = cols // tn
        ahead = [max(LAG, units * per // 7) for units in AHEAD]
        tile = rows * tn * 4
        fixed = 2 * wide * rows * depth * 2 + tile * (2 * per * (2 * 3 + 2) + 2 * (ahead[0] + LAG) + per)
        slots = (VMEM_BYTES - 1_500_000 - fixed) // (4 * tn * depth)
        slots = min(slots, 2 * per)
        if per - max(ahead) >= LAG and slots >= per + 2 and sum(ahead) + per > max(RELAYS)[0]:
            return tn, slots, ahead
    return None


def fused(states, weights, token_ids, lengths, ratio_weight, wide, tn, slots, ahead):
    rows, depth = states[0].shape
    cols = weights[0].shape[1]
    per = cols // tn
    units = 2 * per
    smem = pl.BlockSpec(memory_space=pltpu.SMEM)
    hbm = pl.BlockSpec(memory_space=pl.ANY)
    dma = pltpu.SemaphoreType.DMA
    wire = pltpu.VMEM((units, 2, rows, tn), jnp.bfloat16)
    held = pltpu.VMEM((rows, cols), jnp.bfloat16)
    vmem = pl.BlockSpec(memory_space=pltpu.VMEM)
    return pl.pallas_call(
        functools.partial(kernel, tn, slots, ahead),
        out_shape=(held, held),
        in_specs=[smem, smem] + [hbm] * 7,
        out_specs=(vmem, vmem),
        scratch_shapes=[
            pltpu.VMEM((2, wide, rows, depth), jnp.bfloat16),
            pltpu.VMEM((slots, 2, depth, tn), jnp.bfloat16),
            pltpu.VMEM((ahead[0] + LAG, 2, rows, tn), jnp.float32),
            pltpu.VMEM((units, 2, rows, tn), jnp.float32),
            wire, wire, wire, wire, wire, wire,
            pltpu.VMEM((per, rows, tn), jnp.float32),
            pltpu.VMEM((rows, 1), jnp.float32),
            pltpu.VMEM((rows, 1), jnp.float32),
            pltpu.SMEM(ratio_weight.shape, jnp.float32),
            dma,
            dma((2,)),
            dma((2, 3, wide, max(PIECES))),
            dma((2, wide, max(PIECES))),
            dma((slots, 2)),
            dma((units,)),
            dma((units,)),
            dma((units,)),
            dma((units,)),
            dma((units,)),
            dma((units,)),
        ],
        compiler_params=pltpu.CompilerParams(
            collective_id=0, has_side_effects=True, vmem_limit_bytes=VMEM_BYTES
        ),
        name="rescore",
    )(token_ids, lengths, ratio_weight, *states, *weights)


def local(
    wide,
    narrow,
    target_states,
    source_states,
    target_gate,
    target_up,
    source_gate,
    source_up,
    token_ids,
    lengths,
    ratio_weight,
):
    hidden_cols = target_gate.shape[1]
    own_rows = token_ids.shape[0]
    chosen = plan(target_states, target_gate, wide, narrow)
    if chosen is not None:
        return fused(
            (target_states, source_states),
            (target_gate, target_up, source_gate, source_up),
            token_ids,
            lengths,
            ratio_weight,
            wide,
            *chosen,
        )
    slot_count = own_rows // lengths.shape[0]
    slots = jnp.arange(slot_count, dtype=jnp.int32)
    live = (slots[None, :] < lengths[:, None]).reshape(-1).astype(jnp.float32)
    weight = ratio_weight[token_ids]
    target_terms = pair_project(
        target_gate, target_up, lax.all_gather(target_states, "wide", axis=0, tiled=True)
    )
    source_terms = pair_project(
        source_gate, source_up, lax.all_gather(source_states, "wide", axis=0, tiled=True)
    )
    target_sum, source_sum = (
        lax.psum_scatter(
            target_terms.astype(jnp.bfloat16), "narrow", scatter_dimension=0, tiled=True
        ).astype(jnp.float32),
        lax.psum_scatter(
            source_terms.astype(jnp.bfloat16), "narrow", scatter_dimension=0, tiled=True
        ).astype(jnp.float32),
    )
    target_act = gated(target_sum, hidden_cols)
    source_act = gated(source_sum, hidden_cols)
    target_out = (live[:, None] * target_act).astype(jnp.bfloat16)
    ratio_out = (live[:, None] * (target_act - weight[:, None] * source_act)).astype(jnp.bfloat16)
    return (target_out, ratio_out)


def solution(mesh):
    placed = (
        P(("groups", "wide"), "narrow"),
        P(("groups", "wide"), "narrow"),
        P("narrow", "wide"),
        P("narrow", "wide"),
        P("narrow", "wide"),
        P("narrow", "wide"),
        P(("groups", "narrow")),
        P(("groups", "narrow")),
        P(),
    )
    return jax.shard_map(
        functools.partial(local, mesh.shape["wide"], mesh.shape["narrow"]),
        mesh=mesh,
        in_specs=placed,
        out_specs=(P(("groups", "narrow"), "wide"), P(("groups", "narrow"), "wide")),
        check_vma=False,
    )
```

```python
import functools

import jax
import jax.numpy as jnp
from jax import lax
from jax.experimental import pallas as pl
from jax.experimental.pallas import tpu as pltpu
from jax.sharding import PartitionSpec as P

MESH = pl.DeviceIdType.MESH
VMEM_BYTES = 66_000_000
PIECES = (4, 2)
LAG = 2
AHEAD = (4, 3)
RELAYS = (
    (0, 2, 1, 0, 1), (1, 2, 1, 1, 1), (2, 2, 0, 0, 1), (3, 2, 0, 1, 1),
    (1, 1, 2, 0, -1), (2, 1, 2, 1, -1), (3, 1, 3, 0, -1), (4, 1, 3, 1, -1),
)


def matmul(left, right):
    return jnp.dot(left, right, preferred_element_type=jnp.float32)


def pair_project(w_gate, w_upper, piece):
    return jnp.concatenate([matmul(piece, w_gate), matmul(piece, w_upper)], axis=1)


def gated(summed, hidden_cols):
    return jax.nn.silu(summed[:, :hidden_cols]) * summed[:, hidden_cols:]


def kernel(
    tn, slots, ahead,
    ids_ref, len_ref, table_ref, ts_ref, ss_ref, tg_ref, tu_ref, sg_ref, su_ref,
    t_out, r_out,
    gath, wbuf, far_kept, near_kept, far_send, far_recv, near_send, near_recv, b_send, b_recv,
    kept, live_ref, weight_ref, table,
    table_sem, own_sem, g_send, g_recv, w_sem, fs_sem, fr_sem, ns_sem, nr_sem, bs_sem, br_sem,
):
    w = lax.axis_index("wide")
    n = lax.axis_index("narrow")
    x = n // 2
    c = n % 2
    mate = 2 * x + (1 - c)
    across = 2 * (1 - x) + c
    beside = 2 * (1 - x) + (1 - c)
    toward = 2 * x - 1
    v = x * w + (1 - x) * (3 - w)
    cols = tg_ref.shape[1]
    per = cols // tn
    units = 2 * per
    rows = gath.shape[2]
    depth = gath.shape[3]
    kept_slots = far_kept.shape[0]
    weights = ((tg_ref, tu_ref), (sg_ref, su_ref))

    def block(b):
        return x * b + (1 - x) * (3 - b)

    first = jnp.where(v == 0, block(0), block(1))
    second = jnp.where(v == 0, block(1), block(0))
    leads = across == first

    def weight_copies(u, model, j):
        span = pl.ds(pl.multiple_of(j * tn, tn), tn)
        return [
            pltpu.make_async_copy(weights[model][k].at[:, span], wbuf.at[u % slots, k], w_sem.at[u % slots, k])
            for k in range(2)
        ]

    def load(low, high):
        for u in range(low, high):
            for copy in weight_copies(u, u // per, u % per):
                copy.start()

    own = [
        pltpu.make_async_copy(ref, gath.at[m, w], own_sem.at[m])
        for m, ref in enumerate((ts_ref, ss_ref))
    ]
    for copy in own:
        copy.start()
    load(0, 2)

    barrier = pltpu.get_barrier_semaphore()

    def greet(axis, index):
        pl.semaphore_signal(barrier, inc=1, device_id={axis: index}, device_id_type=MESH)

    for gap in (-2, -1, 1, 2):
        @pl.when(jnp.logical_and(w + gap >= 0, w + gap <= 3))
        def _():
            greet("wide", w + gap)

    greet("narrow", mate)
    greet("narrow", across)
    inner = jnp.logical_and(w > 0, w < 3)
    pl.semaphore_wait(barrier, jnp.where(inner, 5, 4))

    def hop(m, b, p, step):
        size = depth // PIECES[m]
        part = gath.at[m, block(b), :, pl.ds(p * size, size)]
        way = {1: 0, -1: 1, 2: 2, -2: 2}[step]
        return pltpu.make_async_remote_copy(
            src_ref=part, dst_ref=part,
            send_sem=g_send.at[m, way, b, p], recv_sem=g_recv.at[m, b, p],
            device_id={"wide": w + toward * step}, device_id_type=MESH,
        )

    def send(m, b, *steps):
        for p in range(PIECES[m]):
            for step in steps:
                hop(m, b, p, step).start()

    def arrive(m, *blocks):
        for b in blocks:
            for p in range(PIECES[m]):
                hop(m, b, p, 1).wait_recv()

    def relay_piece(m, b, p, step):
        hop(m, b, p, 1).wait_recv()
        hop(m, b, p, step).start()

    def relay(m, b, step):
        for p in range(PIECES[m]):
            relay_piece(m, b, p, step)

    own[0].wait()

    @pl.when(v == 0)
    def _():
        send(0, 0, 1)
        send(0, 0, 2)

    @pl.when(v == 1)
    def _():
        send(0, 1, 1, -1)

    @pl.when(v == 2)
    def _():
        send(0, 2, -1, 1)

    @pl.when(v == 3)
    def _():
        send(0, 3, -1)
        send(0, 3, -2)

    own[1].wait()
    load(2, slots)
    fetch = pltpu.make_async_copy(table_ref, table, table_sem)
    fetch.start()

    @pl.when(v == 0)
    def _():
        send(1, 0, 2)
        send(1, 0, 1)

    @pl.when(v == 1)
    def _():
        relay(0, 2, -1)
        send(1, 1, 1)
        relay(0, 3, -1)
        send(1, 1, -1)

    @pl.when(v == 2)
    def _():
        relay(0, 1, 1)
        send(1, 2, -1)
        relay(0, 0, 1)

    @pl.when(v == 3)
    def _():
        send(1, 3, -2)
        send(1, 3, -1)
        arrive(0, 1)

    def relays(step):
        for at, where, b, p, way in RELAYS:
            @pl.when(jnp.logical_and(step == at, v == where))
            def _():
                relay_piece(1, b, p, way)

        @pl.when(jnp.logical_and(step == max(RELAYS)[0], v == 2))
        def _():
            send(1, 2, 1)

    def far_copy(u):
        return pltpu.make_async_remote_copy(
            src_ref=far_send.at[u], dst_ref=far_recv.at[u],
            send_sem=fs_sem.at[u], recv_sem=fr_sem.at[u],
            device_id={"narrow": mate}, device_id_type=MESH,
        )

    def near_copy(u):
        return pltpu.make_async_remote_copy(
            src_ref=near_send.at[u], dst_ref=near_recv.at[u],
            send_sem=ns_sem.at[u], recv_sem=nr_sem.at[u],
            device_id={"narrow": mate}, device_id_type=MESH,
        )

    def b_copy(u):
        return pltpu.make_async_remote_copy(
            src_ref=b_send.at[u], dst_ref=b_recv.at[u],
            send_sem=bs_sem.at[u], recv_sem=br_sem.at[u],
            device_id={"narrow": across}, device_id_type=MESH,
        )

    def cross(u):
        far_copy(u).wait_recv()
        for k in range(2):
            total = far_kept[u % kept_slots, k] + far_recv[u, k].astype(jnp.float32)
            b_send[u, k] = total.astype(jnp.bfloat16)
        b_copy(u).start()

    def tokens(model, *blocks):
        return jnp.concatenate([gath[model, i] for i in blocks], axis=0)

    def await_weights(u, model, j):
        for copy in weight_copies(u, model, j):
            copy.wait()

    def keep_far(u, k, out):
        far_kept[u % kept_slots, k] = out

    def give_far(u, k, out):
        far_send[u, k] = out.astype(jnp.bfloat16)

    def share_near(u, k, out):
        near_kept[u, k] = out[:rows]
        near_send[u, k] = out[rows:].astype(jnp.bfloat16)

    def refill(u):
        @pl.when(u + slots < units)
        def _():
            for copy in weight_copies(u + slots, 1, u + slots - per):
                copy.start()

    def phase(low, high, step0, body):
        def run(j, carry):
            relays(step0 + j - low)
            body(j)
            return carry
        lax.fori_loop(low, high, run, 0)
        return step0 + high - low

    def one_block(u, k, out, mine):
        @pl.when(mine)
        def _():
            keep_far(u, k, out)

        @pl.when(jnp.logical_not(mine))
        def _():
            give_far(u, k, out)

    def pass_on(u, mine):
        @pl.when(jnp.logical_not(mine))
        def _():
            far_copy(u).start()

        @pl.when(jnp.logical_and(mine, u >= LAG))
        def _():
            cross(u - LAG)

    def early(u):
        await_weights(u, 0, u)
        left = gath[0, first]
        for k in range(2):
            one_block(u, k, matmul(left, wbuf[u % slots, k]), leads)
        pass_on(u, leads)

    def rest(u):
        left = tokens(0, second, n, mate)
        for k in range(2):
            out = matmul(left, wbuf[u % slots, k])
            one_block(u, k, out[:rows], jnp.logical_not(leads))
            share_near(u, k, out[rows:])
        near_copy(u).start()
        pass_on(u, jnp.logical_not(leads))

        @pl.when(jnp.logical_and(leads, u < LAG))
        def _():
            cross(ahead[0] - LAG + u)

        refill(u)

    def whole(u, model):
        await_weights(u, model, u - model * per)
        left = tokens(model, across, beside, n, mate)
        for k in range(2):
            out = matmul(left, wbuf[u % slots, k])
            keep_far(u, k, out[:rows])
            give_far(u, k, out[rows:2 * rows])
            share_near(u, k, out[2 * rows:])
        far_copy(u).start()
        near_copy(u).start()

    def target(u):
        whole(u, 0)
        refill(u)

        @pl.when(jnp.logical_or(u >= ahead[0] + LAG, jnp.logical_not(leads)))
        def _():
            cross(u - LAG)

    def summed(u, k):
        near = near_kept[u, k] + near_recv[u, k].astype(jnp.float32)
        return near + b_recv[u, k].astype(jnp.float32)

    def activation(u):
        near_copy(u).wait_recv()
        b_copy(u).wait_recv()
        gate = summed(u, 0)
        return gate / (1.0 + jnp.exp(-gate)) * summed(u, 1)

    def finish_target(j):
        act = activation(j)
        kept[j] = act
        t_out[:, pl.ds(pl.multiple_of(j * tn, tn), tn)] = (live_ref[...] * act).astype(t_out.dtype)

    def finish_ratio(j, carry):
        act = activation(per + j)
        ratio = live_ref[...] * (kept[j] - weight_ref[...] * act)
        r_out[:, pl.ds(pl.multiple_of(j * tn, tn), tn)] = ratio.astype(r_out.dtype)
        return carry

    def source_far(j):
        u = per + j
        await_weights(u, 1, j)
        left = tokens(1, across, beside)
        for k in range(2):
            out = matmul(left, wbuf[u % slots, k])
            keep_far(u, k, out[:rows])
            give_far(u, k, out[rows:])
        far_copy(u).start()
        cross(u - LAG)

    def source_all(j):
        whole(per + j, 1)
        cross(per + j - LAG)
        finish_target(j - ahead[1])

    def source_near(j):
        u = per + j
        left = tokens(1, n, mate)
        for k in range(2):
            share_near(u, k, matmul(left, wbuf[u % slots, k]))
        near_copy(u).start()

        @pl.when(j < LAG)
        def _():
            cross(units - LAG + j)

        finish_target(per - ahead[1] + j)

    row = lax.broadcasted_iota(jnp.int32, (rows, 1), 0)
    hlen = rows // len_ref.shape[0]
    lived = jnp.zeros((rows, 1), jnp.float32)
    for h in range(len_ref.shape[0]):
        inside = jnp.logical_and(row >= h * hlen, row < h * hlen + len_ref[h])
        lived = jnp.where(inside, 1.0, lived)
    live_ref[...] = lived

    step = phase(0, ahead[0], 0, early)

    @pl.when(v == 0)
    def _():
        arrive(0, 1, 2, 3)

    @pl.when(v == 1)
    def _():
        arrive(0, 0)

    @pl.when(v == 2)
    def _():
        arrive(0, 3)

    @pl.when(v == 3)
    def _():
        arrive(0, 2, 0)

    step = phase(0, ahead[0], step, rest)
    step = phase(ahead[0], per, step, target)

    @pl.when(v == 0)
    def _():
        arrive(1, 1)

    @pl.when(v == 1)
    def _():
        arrive(1, 0)

    @pl.when(v == 3)
    def _():
        arrive(1, 1, 0)

    step = phase(0, ahead[1], step, source_far)

    @pl.when(v == 0)
    def _():
        arrive(1, 2, 3)

    @pl.when(v == 2)
    def _():
        arrive(1, 3)

    @pl.when(v == 3)
    def _():
        arrive(1, 2)

    step = phase(ahead[1], per, step, source_all)
    step = phase(0, ahead[1], step, source_near)

    fetch.wait()
    picked = jnp.zeros((rows, 1), jnp.float32)
    for i in range(rows):
        picked = jnp.where(row == i, table[ids_ref[i]], picked)
    weight_ref[...] = picked
    lax.fori_loop(0, per, finish_ratio, 0)

    def drain(u, carry):
        far_copy(u).wait_send()
        near_copy(u).wait_send()
        b_copy(u).wait_send()
        return carry

    lax.fori_loop(0, units, drain, 0)
    for m in range(2):
        for where, b, way in ((0, 0, 1), (0, 0, 2), (1, 1, 1), (1, 1, -1), (1, 2, -1), (1, 3, -1),
                              (2, 2, -1), (2, 2, 1), (2, 1, 1), (2, 0, 1), (3, 3, -1), (3, 3, -2)):
            @pl.when(v == where)
            def _():
                for p in range(PIECES[m]):
                    hop(m, b, p, way).wait_send()


def plan(states, weights, wide, narrow):
    depth, cols = weights.shape
    rows = states.shape[0]
    if narrow != 4 or wide != 4 or rows % 16 or depth % (128 * max(PIECES)):
        return None
    for tn in (512, 256):
        if cols % tn or cols // tn < 3:
            continue
        per = cols // tn
        ahead = [max(LAG, units * per // 7) for units in AHEAD]
        tile = rows * tn * 4
        fixed = 2 * wide * rows * depth * 2 + tile * (2 * per * (2 * 3 + 2) + 2 * (ahead[0] + LAG) + per)
        slots = (VMEM_BYTES - 1_500_000 - fixed) // (4 * tn * depth)
        slots = min(slots, 2 * per)
        if per - max(ahead) >= LAG and slots >= per + 2 and sum(ahead) + per > max(RELAYS)[0]:
            return tn, slots, ahead
    return None


def fused(states, weights, token_ids, lengths, ratio_weight, wide, tn, slots, ahead):
    rows, depth = states[0].shape
    cols = weights[0].shape[1]
    per = cols // tn
    units = 2 * per
    smem = pl.BlockSpec(memory_space=pltpu.SMEM)
    hbm = pl.BlockSpec(memory_space=pl.ANY)
    dma = pltpu.SemaphoreType.DMA
    wire = pltpu.VMEM((units, 2, rows, tn), jnp.bfloat16)
    held = pltpu.VMEM((rows, cols), jnp.bfloat16)
    vmem = pl.BlockSpec(memory_space=pltpu.VMEM)
    return pl.pallas_call(
        functools.partial(kernel, tn, slots, ahead),
        out_shape=(held, held),
        in_specs=[smem, smem] + [hbm] * 7,
        out_specs=(vmem, vmem),
        scratch_shapes=[
            pltpu.VMEM((2, wide, rows, depth), jnp.bfloat16),
            pltpu.VMEM((slots, 2, depth, tn), jnp.bfloat16),
            pltpu.VMEM((ahead[0] + LAG, 2, rows, tn), jnp.float32),
            pltpu.VMEM((units, 2, rows, tn), jnp.float32),
            wire, wire, wire, wire, wire, wire,
            pltpu.VMEM((per, rows, tn), jnp.float32),
            pltpu.VMEM((rows, 1), jnp.float32),
            pltpu.VMEM((rows, 1), jnp.float32),
            pltpu.SMEM(ratio_weight.shape, jnp.float32),
            dma,
            dma((2,)),
            dma((2, 3, wide, max(PIECES))),
            dma((2, wide, max(PIECES))),
            dma((slots, 2)),
            dma((units,)),
            dma((units,)),
            dma((units,)),
            dma((units,)),
            dma((units,)),
            dma((units,)),
        ],
        compiler_params=pltpu.CompilerParams(
            collective_id=0, has_side_effects=True, vmem_limit_bytes=VMEM_BYTES
        ),
        name="rescore",
    )(token_ids, lengths, ratio_weight, *states, *weights)


def local(
    wide,
    narrow,
    target_states,
    source_states,
    target_gate,
    target_up,
    source_gate,
    source_up,
    token_ids,
    lengths,
    ratio_weight,
):
    hidden_cols = target_gate.shape[1]
    own_rows = token_ids.shape[0]
    chosen = plan(target_states, target_gate, wide, narrow)
    if chosen is not None:
        return fused(
            (target_states, source_states),
            (target_gate, target_up, source_gate, source_up),
            token_ids,
            lengths,
            ratio_weight,
            wide,
            *chosen,
        )
    slot_count = own_rows // lengths.shape[0]
    slots = jnp.arange(slot_count, dtype=jnp.int32)
    live = (slots[None, :] < lengths[:, None]).reshape(-1).astype(jnp.float32)
    weight = ratio_weight[token_ids]
    target_terms = pair_project(
        target_gate, target_up, lax.all_gather(target_states, "wide", axis=0, tiled=True)
    )
    source_terms = pair_project(
        source_gate, source_up, lax.all_gather(source_states, "wide", axis=0, tiled=True)
    )
    target_sum, source_sum = (
        lax.psum_scatter(
            target_terms.astype(jnp.bfloat16), "narrow", scatter_dimension=0, tiled=True
        ).astype(jnp.float32),
        lax.psum_scatter(
            source_terms.astype(jnp.bfloat16), "narrow", scatter_dimension=0, tiled=True
        ).astype(jnp.float32),
    )
    target_act = gated(target_sum, hidden_cols)
    source_act = gated(source_sum, hidden_cols)
    target_out = (live[:, None] * target_act).astype(jnp.bfloat16)
    ratio_out = (live[:, None] * (target_act - weight[:, None] * source_act)).astype(jnp.bfloat16)
    return (target_out, ratio_out)


def solution(mesh):
    placed = (
        P(("groups", "wide"), "narrow"),
        P(("groups", "wide"), "narrow"),
        P("narrow", "wide"),
        P("narrow", "wide"),
        P("narrow", "wide"),
        P("narrow", "wide"),
        P(("groups", "narrow")),
        P(("groups", "narrow")),
        P(),
    )
    return jax.shard_map(
        functools.partial(local, mesh.shape["wide"], mesh.shape["narrow"]),
        mesh=mesh,
        in_specs=placed,
        out_specs=(P(("groups", "narrow"), "wide"), P(("groups", "narrow"), "wide")),
        check_vma=False,
    )
```

```python
import functools

import jax
import jax.numpy as jnp
from jax import lax
from jax.experimental import pallas as pl
from jax.experimental.pallas import tpu as pltpu
from jax.sharding import PartitionSpec as P

MESH = pl.DeviceIdType.MESH
VMEM_BYTES = 66_000_000
PIECES = (4, 2)
LAG = 2
AHEAD = (4, 3)
RELAYS = (
    (0, 1, 0, 3, 0, -1), (1, 1, 0, 3, 1, -1), (2, 1, 0, 3, 2, -1), (3, 1, 0, 3, 3, -1),
    (0, 2, 0, 0, 0, 1), (1, 2, 0, 0, 1, 1), (2, 2, 0, 0, 2, 1), (3, 2, 0, 0, 3, 1),
    (5, 2, 1, 1, 0, 1), (6, 2, 1, 1, 1, 1), (7, 2, 1, 0, 0, 1), (8, 2, 1, 0, 1, 1),
    (5, 1, 1, 2, 0, -1), (6, 1, 1, 2, 1, -1), (7, 1, 1, 3, 0, -1), (8, 1, 1, 3, 1, -1),
)


def matmul(left, right):
    return jnp.dot(left, right, preferred_element_type=jnp.float32)


def pair_project(w_gate, w_upper, piece):
    return jnp.concatenate([matmul(piece, w_gate), matmul(piece, w_upper)], axis=1)


def gated(summed, hidden_cols):
    return jax.nn.silu(summed[:, :hidden_cols]) * summed[:, hidden_cols:]


def kernel(
    tn, slots, ahead,
    ids_ref, len_ref, table_ref, ts_ref, ss_ref, tg_ref, tu_ref, sg_ref, su_ref,
    t_out, r_out,
    gath, wbuf, far_kept, near_kept, far_send, far_recv, near_send, near_recv, b_send, b_recv,
    kept, live_ref, weight_ref, table,
    table_sem, own_sem, g_send, g_recv, w_sem, fs_sem, fr_sem, ns_sem, nr_sem, bs_sem, br_sem,
):
    w = lax.axis_index("wide")
    n = lax.axis_index("narrow")
    x = n // 2
    c = n % 2
    mate = 2 * x + (1 - c)
    across = 2 * (1 - x) + c
    beside = 2 * (1 - x) + (1 - c)
    toward = 2 * x - 1
    v = x * w + (1 - x) * (3 - w)
    cols = tg_ref.shape[1]
    per = cols // tn
    units = 2 * per
    rows = gath.shape[2]
    depth = gath.shape[3]
    kept_slots = far_kept.shape[0]
    weights = ((tg_ref, tu_ref), (sg_ref, su_ref))

    def block(b):
        return x * b + (1 - x) * (3 - b)

    first = jnp.where(v == 0, block(0), block(1))
    second = jnp.where(v == 0, block(1), block(0))
    leads = across == first

    def weight_copies(u, model, j):
        span = pl.ds(pl.multiple_of(j * tn, tn), tn)
        return [
            pltpu.make_async_copy(weights[model][k].at[:, span], wbuf.at[u % slots, k], w_sem.at[u % slots, k])
            for k in range(2)
        ]

    def load(low, high):
        for u in range(low, high):
            for copy in weight_copies(u, u // per, u % per):
                copy.start()

    own = [
        pltpu.make_async_copy(ref, gath.at[m, w], own_sem.at[m])
        for m, ref in enumerate((ts_ref, ss_ref))
    ]
    for copy in own:
        copy.start()
    load(0, 2)

    barrier = pltpu.get_barrier_semaphore()

    def greet(axis, index):
        pl.semaphore_signal(barrier, inc=1, device_id={axis: index}, device_id_type=MESH)

    for gap in (-2, -1, 1, 2):
        @pl.when(jnp.logical_and(w + gap >= 0, w + gap <= 3))
        def _():
            greet("wide", w + gap)

    greet("narrow", mate)
    greet("narrow", across)
    inner = jnp.logical_and(w > 0, w < 3)
    pl.semaphore_wait(barrier, jnp.where(inner, 5, 4))

    def hop(m, b, p, step):
        size = depth // PIECES[m]
        part = gath.at[m, block(b), :, pl.ds(p * size, size)]
        way = {1: 0, -1: 1, 2: 2, -2: 2}[step]
        return pltpu.make_async_remote_copy(
            src_ref=part, dst_ref=part,
            send_sem=g_send.at[m, way, b, p], recv_sem=g_recv.at[m, b, p],
            device_id={"wide": w + toward * step}, device_id_type=MESH,
        )

    def send(m, b, *steps):
        for p in range(PIECES[m]):
            for step in steps:
                hop(m, b, p, step).start()

    def arrive(m, *blocks):
        for b in blocks:
            for p in range(PIECES[m]):
                hop(m, b, p, 1).wait_recv()

    def relay_piece(m, b, p, step):
        hop(m, b, p, 1).wait_recv()
        hop(m, b, p, step).start()

    def relay(m, b, step):
        for p in range(PIECES[m]):
            relay_piece(m, b, p, step)

    own[0].wait()

    @pl.when(v == 0)
    def _():
        send(0, 0, 1)
        send(0, 0, 2)

    @pl.when(v == 1)
    def _():
        send(0, 1, 1, -1)

    @pl.when(v == 2)
    def _():
        send(0, 2, -1, 1)

    @pl.when(v == 3)
    def _():
        send(0, 3, -1)
        send(0, 3, -2)

    own[1].wait()
    load(2, slots)
    fetch = pltpu.make_async_copy(table_ref, table, table_sem)
    fetch.start()

    @pl.when(v == 0)
    def _():
        send(1, 0, 2)
        send(1, 0, 1)

    @pl.when(v == 1)
    def _():
        relay(0, 2, -1)
        send(1, 1, 1)

    @pl.when(v == 2)
    def _():
        relay(0, 1, 1)
        send(1, 2, -1)

    @pl.when(v == 3)
    def _():
        send(1, 3, -2)
        send(1, 3, -1)
        arrive(0, 1)

    def relays(step):
        for at, where, m, b, p, way in RELAYS:
            @pl.when(jnp.logical_and(step == at, v == where))
            def _():
                relay_piece(m, b, p, way)

        @pl.when(jnp.logical_and(step == PIECES[0], v == 1))
        def _():
            send(1, 1, -1)

        @pl.when(jnp.logical_and(step == 8, v == 2))
        def _():
            send(1, 2, 1)

    def far_copy(u):
        return pltpu.make_async_remote_copy(
            src_ref=far_send.at[u], dst_ref=far_recv.at[u],
            send_sem=fs_sem.at[u], recv_sem=fr_sem.at[u],
            device_id={"narrow": mate}, device_id_type=MESH,
        )

    def near_copy(u):
        return pltpu.make_async_remote_copy(
            src_ref=near_send.at[u], dst_ref=near_recv.at[u],
            send_sem=ns_sem.at[u], recv_sem=nr_sem.at[u],
            device_id={"narrow": mate}, device_id_type=MESH,
        )

    def b_copy(u):
        return pltpu.make_async_remote_copy(
            src_ref=b_send.at[u], dst_ref=b_recv.at[u],
            send_sem=bs_sem.at[u], recv_sem=br_sem.at[u],
            device_id={"narrow": across}, device_id_type=MESH,
        )

    def cross(u):
        far_copy(u).wait_recv()
        for k in range(2):
            total = far_kept[u % kept_slots, k] + far_recv[u, k].astype(jnp.float32)
            b_send[u, k] = total.astype(jnp.bfloat16)
        b_copy(u).start()

    def tokens(model, *blocks):
        return jnp.concatenate([gath[model, i] for i in blocks], axis=0)

    def await_weights(u, model, j):
        for copy in weight_copies(u, model, j):
            copy.wait()

    def keep_far(u, k, out):
        far_kept[u % kept_slots, k] = out

    def give_far(u, k, out):
        far_send[u, k] = out.astype(jnp.bfloat16)

    def share_near(u, k, out):
        near_kept[u, k] = out[:rows]
        near_send[u, k] = out[rows:].astype(jnp.bfloat16)

    def refill(u):
        @pl.when(u + slots < units)
        def _():
            for copy in weight_copies(u + slots, 1, u + slots - per):
                copy.start()

    def phase(low, high, step0, body):
        def run(j, carry):
            relays(step0 + j - low)
            body(j)
            return carry
        lax.fori_loop(low, high, run, 0)
        return step0 + high - low

    def one_block(u, k, out, mine):
        @pl.when(mine)
        def _():
            keep_far(u, k, out)

        @pl.when(jnp.logical_not(mine))
        def _():
            give_far(u, k, out)

    def pass_on(u, mine):
        @pl.when(jnp.logical_not(mine))
        def _():
            far_copy(u).start()

        @pl.when(jnp.logical_and(mine, u >= LAG))
        def _():
            cross(u - LAG)

    def early(u):
        await_weights(u, 0, u)
        left = gath[0, first]
        for k in range(2):
            one_block(u, k, matmul(left, wbuf[u % slots, k]), leads)
        pass_on(u, leads)

    def rest(u):
        left = tokens(0, second, n, mate)
        for k in range(2):
            out = matmul(left, wbuf[u % slots, k])
            one_block(u, k, out[:rows], jnp.logical_not(leads))
            share_near(u, k, out[rows:])
        near_copy(u).start()
        pass_on(u, jnp.logical_not(leads))

        @pl.when(jnp.logical_and(leads, u < LAG))
        def _():
            cross(ahead[0] - LAG + u)

        refill(u)

    def whole(u, model):
        await_weights(u, model, u - model * per)
        left = tokens(model, across, beside, n, mate)
        for k in range(2):
            out = matmul(left, wbuf[u % slots, k])
            keep_far(u, k, out[:rows])
            give_far(u, k, out[rows:2 * rows])
            share_near(u, k, out[2 * rows:])
        far_copy(u).start()
        near_copy(u).start()

    def target(u):
        whole(u, 0)
        refill(u)

        @pl.when(jnp.logical_or(u >= ahead[0] + LAG, jnp.logical_not(leads)))
        def _():
            cross(u - LAG)

    def summed(u, k):
        near = near_kept[u, k] + near_recv[u, k].astype(jnp.float32)
        return near + b_recv[u, k].astype(jnp.float32)

    def activation(u):
        near_copy(u).wait_recv()
        b_copy(u).wait_recv()
        gate = summed(u, 0)
        return gate / (1.0 + jnp.exp(-gate)) * summed(u, 1)

    def finish_target(j):
        act = activation(j)
        kept[j] = act
        t_out[:, pl.ds(pl.multiple_of(j * tn, tn), tn)] = (live_ref[...] * act).astype(t_out.dtype)

    def finish_ratio(j, carry):
        act = activation(per + j)
        ratio = live_ref[...] * (kept[j] - weight_ref[...] * act)
        r_out[:, pl.ds(pl.multiple_of(j * tn, tn), tn)] = ratio.astype(r_out.dtype)
        return carry

    def source_far(j):
        u = per + j
        await_weights(u, 1, j)
        left = tokens(1, across, beside)
        for k in range(2):
            out = matmul(left, wbuf[u % slots, k])
            keep_far(u, k, out[:rows])
            give_far(u, k, out[rows:])
        far_copy(u).start()
        cross(u - LAG)

    def source_all(j):
        whole(per + j, 1)
        cross(per + j - LAG)
        finish_target(j - ahead[1])

    def source_near(j):
        u = per + j
        left = tokens(1, n, mate)
        for k in range(2):
            share_near(u, k, matmul(left, wbuf[u % slots, k]))
        near_copy(u).start()

        @pl.when(j < LAG)
        def _():
            cross(units - LAG + j)

        finish_target(per - ahead[1] + j)

    row = lax.broadcasted_iota(jnp.int32, (rows, 1), 0)
    hlen = rows // len_ref.shape[0]
    lived = jnp.zeros((rows, 1), jnp.float32)
    for h in range(len_ref.shape[0]):
        inside = jnp.logical_and(row >= h * hlen, row < h * hlen + len_ref[h])
        lived = jnp.where(inside, 1.0, lived)
    live_ref[...] = lived

    step = phase(0, ahead[0], 0, early)

    @pl.when(v == 0)
    def _():
        arrive(0, 1, 2, 3)

    @pl.when(v == 1)
    def _():
        arrive(0, 0)

    @pl.when(v == 2)
    def _():
        arrive(0, 3)

    @pl.when(v == 3)
    def _():
        arrive(0, 2, 0)

    step = phase(0, ahead[0], step, rest)
    step = phase(ahead[0], per, step, target)

    @pl.when(v == 0)
    def _():
        arrive(1, 1)

    @pl.when(v == 1)
    def _():
        arrive(1, 0)

    @pl.when(v == 3)
    def _():
        arrive(1, 1, 0)

    step = phase(0, ahead[1], step, source_far)

    @pl.when(v == 0)
    def _():
        arrive(1, 2, 3)

    @pl.when(v == 2)
    def _():
        arrive(1, 3)

    @pl.when(v == 3)
    def _():
        arrive(1, 2)

    step = phase(ahead[1], per, step, source_all)
    step = phase(0, ahead[1], step, source_near)

    fetch.wait()
    picked = jnp.zeros((rows, 1), jnp.float32)
    for i in range(rows):
        picked = jnp.where(row == i, table[ids_ref[i]], picked)
    weight_ref[...] = picked
    lax.fori_loop(0, per, finish_ratio, 0)

    def drain(u, carry):
        far_copy(u).wait_send()
        near_copy(u).wait_send()
        b_copy(u).wait_send()
        return carry

    lax.fori_loop(0, units, drain, 0)
    for m in range(2):
        for where, b, way in ((0, 0, 1), (0, 0, 2), (1, 1, 1), (1, 1, -1), (1, 2, -1), (1, 3, -1),
                              (2, 2, -1), (2, 2, 1), (2, 1, 1), (2, 0, 1), (3, 3, -1), (3, 3, -2)):
            @pl.when(v == where)
            def _():
                for p in range(PIECES[m]):
                    hop(m, b, p, way).wait_send()


def plan(states, weights, wide, narrow):
    depth, cols = weights.shape
    rows = states.shape[0]
    if narrow != 4 or wide != 4 or rows % 16 or depth % (128 * max(PIECES)):
        return None
    for tn in (512, 256):
        if cols % tn or cols // tn < 3:
            continue
        per = cols // tn
        ahead = [max(LAG, units * per // 7) for units in AHEAD]
        tile = rows * tn * 4
        fixed = 2 * wide * rows * depth * 2 + tile * (2 * per * (2 * 3 + 2) + 2 * (ahead[0] + LAG) + per)
        slots = (VMEM_BYTES - 1_500_000 - fixed) // (4 * tn * depth)
        slots = min(slots, 2 * per)
        if per - max(ahead) >= LAG and slots >= per + 2 and ahead[0] >= PIECES[0] and ahead[0] + per > max(RELAYS)[0]:
            return tn, slots, ahead
    return None


def fused(states, weights, token_ids, lengths, ratio_weight, wide, tn, slots, ahead):
    rows, depth = states[0].shape
    cols = weights[0].shape[1]
    per = cols // tn
    units = 2 * per
    smem = pl.BlockSpec(memory_space=pltpu.SMEM)
    hbm = pl.BlockSpec(memory_space=pl.ANY)
    dma = pltpu.SemaphoreType.DMA
    wire = pltpu.VMEM((units, 2, rows, tn), jnp.bfloat16)
    held = pltpu.VMEM((rows, cols), jnp.bfloat16)
    vmem = pl.BlockSpec(memory_space=pltpu.VMEM)
    return pl.pallas_call(
        functools.partial(kernel, tn, slots, ahead),
        out_shape=(held, held),
        in_specs=[smem, smem] + [hbm] * 7,
        out_specs=(vmem, vmem),
        scratch_shapes=[
            pltpu.VMEM((2, wide, rows, depth), jnp.bfloat16),
            pltpu.VMEM((slots, 2, depth, tn), jnp.bfloat16),
            pltpu.VMEM((ahead[0] + LAG, 2, rows, tn), jnp.float32),
            pltpu.VMEM((units, 2, rows, tn), jnp.float32),
            wire, wire, wire, wire, wire, wire,
            pltpu.VMEM((per, rows, tn), jnp.float32),
            pltpu.VMEM((rows, 1), jnp.float32),
            pltpu.VMEM((rows, 1), jnp.float32),
            pltpu.SMEM(ratio_weight.shape, jnp.float32),
            dma,
            dma((2,)),
            dma((2, 3, wide, max(PIECES))),
            dma((2, wide, max(PIECES))),
            dma((slots, 2)),
            dma((units,)),
            dma((units,)),
            dma((units,)),
            dma((units,)),
            dma((units,)),
            dma((units,)),
        ],
        compiler_params=pltpu.CompilerParams(
            collective_id=0, has_side_effects=True, vmem_limit_bytes=VMEM_BYTES
        ),
        name="rescore",
    )(token_ids, lengths, ratio_weight, *states, *weights)


def local(
    wide,
    narrow,
    target_states,
    source_states,
    target_gate,
    target_up,
    source_gate,
    source_up,
    token_ids,
    lengths,
    ratio_weight,
):
    hidden_cols = target_gate.shape[1]
    own_rows = token_ids.shape[0]
    chosen = plan(target_states, target_gate, wide, narrow)
    if chosen is not None:
        return fused(
            (target_states, source_states),
            (target_gate, target_up, source_gate, source_up),
            token_ids,
            lengths,
            ratio_weight,
            wide,
            *chosen,
        )
    slot_count = own_rows // lengths.shape[0]
    slots = jnp.arange(slot_count, dtype=jnp.int32)
    live = (slots[None, :] < lengths[:, None]).reshape(-1).astype(jnp.float32)
    weight = ratio_weight[token_ids]
    target_terms = pair_project(
        target_gate, target_up, lax.all_gather(target_states, "wide", axis=0, tiled=True)
    )
    source_terms = pair_project(
        source_gate, source_up, lax.all_gather(source_states, "wide", axis=0, tiled=True)
    )
    target_sum, source_sum = (
        lax.psum_scatter(
            target_terms.astype(jnp.bfloat16), "narrow", scatter_dimension=0, tiled=True
        ).astype(jnp.float32),
        lax.psum_scatter(
            source_terms.astype(jnp.bfloat16), "narrow", scatter_dimension=0, tiled=True
        ).astype(jnp.float32),
    )
    target_act = gated(target_sum, hidden_cols)
    source_act = gated(source_sum, hidden_cols)
    target_out = (live[:, None] * target_act).astype(jnp.bfloat16)
    ratio_out = (live[:, None] * (target_act - weight[:, None] * source_act)).astype(jnp.bfloat16)
    return (target_out, ratio_out)


def solution(mesh):
    placed = (
        P(("groups", "wide"), "narrow"),
        P(("groups", "wide"), "narrow"),
        P("narrow", "wide"),
        P("narrow", "wide"),
        P("narrow", "wide"),
        P("narrow", "wide"),
        P(("groups", "narrow")),
        P(("groups", "narrow")),
        P(),
    )
    return jax.shard_map(
        functools.partial(local, mesh.shape["wide"], mesh.shape["narrow"]),
        mesh=mesh,
        in_specs=placed,
        out_specs=(P(("groups", "narrow"), "wide"), P(("groups", "narrow"), "wide")),
        check_vma=False,
    )
```

```python
import functools

import jax
import jax.numpy as jnp
from jax import lax
from jax.experimental import pallas as pl
from jax.experimental.pallas import tpu as pltpu
from jax.sharding import PartitionSpec as P

MESH = pl.DeviceIdType.MESH
VMEM_BYTES = 66_000_000
PIECES = (4, 2)
LAG = 2
AHEAD = (4, 2)
RELAYS = (
    (2, 2, 1, 0, 1), (4, 2, 1, 1, 1), (5, 2, 0, 0, 1), (7, 2, 0, 1, 1),
    (4, 1, 2, 0, -1), (5, 1, 2, 1, -1), (6, 1, 3, 0, -1), (7, 1, 3, 1, -1),
)


def matmul(left, right):
    return jnp.dot(left, right, preferred_element_type=jnp.float32)


def pair_project(w_gate, w_upper, piece):
    return jnp.concatenate([matmul(piece, w_gate), matmul(piece, w_upper)], axis=1)


def gated(summed, hidden_cols):
    return jax.nn.silu(summed[:, :hidden_cols]) * summed[:, hidden_cols:]


def kernel(
    tn, slots, ahead,
    ids_ref, len_ref, table_ref, ts_ref, ss_ref, tg_ref, tu_ref, sg_ref, su_ref,
    t_out, r_out,
    gath, wbuf, far_kept, near_kept, far_send, far_recv, near_send, near_recv, b_send, b_recv,
    kept, live_ref, weight_ref, table,
    table_sem, own_sem, g_send, g_recv, w_sem, fs_sem, fr_sem, ns_sem, nr_sem, bs_sem, br_sem,
):
    w = lax.axis_index("wide")
    n = lax.axis_index("narrow")
    x = n // 2
    c = n % 2
    mate = 2 * x + (1 - c)
    across = 2 * (1 - x) + c
    beside = 2 * (1 - x) + (1 - c)
    toward = 2 * x - 1
    v = x * w + (1 - x) * (3 - w)
    cols = tg_ref.shape[1]
    per = cols // tn
    units = 2 * per
    rows = gath.shape[2]
    depth = gath.shape[3]
    kept_slots = far_kept.shape[0]
    weights = ((tg_ref, tu_ref), (sg_ref, su_ref))

    def block(b):
        return x * b + (1 - x) * (3 - b)

    first = jnp.where(v == 0, block(0), block(1))
    second = jnp.where(v == 0, block(1), block(0))
    leads = across == first

    def weight_copies(u, model, j):
        span = pl.ds(pl.multiple_of(j * tn, tn), tn)
        return [
            pltpu.make_async_copy(weights[model][k].at[:, span], wbuf.at[u % slots, k], w_sem.at[u % slots, k])
            for k in range(2)
        ]

    def load(low, high):
        for u in range(low, high):
            for copy in weight_copies(u, u // per, u % per):
                copy.start()

    own = [
        pltpu.make_async_copy(ref, gath.at[m, w], own_sem.at[m])
        for m, ref in enumerate((ts_ref, ss_ref))
    ]
    for copy in own:
        copy.start()
    load(0, 2)

    barrier = pltpu.get_barrier_semaphore()

    def greet(axis, index):
        pl.semaphore_signal(barrier, inc=1, device_id={axis: index}, device_id_type=MESH)

    for gap in (-2, -1, 1, 2):
        @pl.when(jnp.logical_and(w + gap >= 0, w + gap <= 3))
        def _():
            greet("wide", w + gap)

    greet("narrow", mate)
    greet("narrow", across)
    inner = jnp.logical_and(w > 0, w < 3)
    pl.semaphore_wait(barrier, jnp.where(inner, 5, 4))

    def hop(m, b, p, step):
        size = depth // PIECES[m]
        part = gath.at[m, block(b), :, pl.ds(p * size, size)]
        way = {1: 0, -1: 1, 2: 2, -2: 2}[step]
        return pltpu.make_async_remote_copy(
            src_ref=part, dst_ref=part,
            send_sem=g_send.at[m, way, b, p], recv_sem=g_recv.at[m, b, p],
            device_id={"wide": w + toward * step}, device_id_type=MESH,
        )

    def send(m, b, *steps):
        for p in range(PIECES[m]):
            for step in steps:
                hop(m, b, p, step).start()

    def arrive(m, *blocks):
        for b in blocks:
            for p in range(PIECES[m]):
                hop(m, b, p, 1).wait_recv()

    def relay_piece(m, b, p, step):
        hop(m, b, p, 1).wait_recv()
        hop(m, b, p, step).start()

    def relay(m, b, step):
        for p in range(PIECES[m]):
            relay_piece(m, b, p, step)

    own[0].wait()

    @pl.when(v == 0)
    def _():
        send(0, 0, 1)
        send(0, 0, 2)

    @pl.when(v == 1)
    def _():
        send(0, 1, 1, -1)

    @pl.when(v == 2)
    def _():
        send(0, 2, -1, 1)

    @pl.when(v == 3)
    def _():
        send(0, 3, -1)
        send(0, 3, -2)

    own[1].wait()
    load(2, slots)
    fetch = pltpu.make_async_copy(table_ref, table, table_sem)
    fetch.start()

    @pl.when(v == 0)
    def _():
        send(1, 0, 2)
        send(1, 0, 1)

    @pl.when(v == 1)
    def _():
        relay(0, 2, -1)
        send(1, 1, 1)
        relay(0, 3, -1)
        send(1, 1, -1)

    @pl.when(v == 2)
    def _():
        relay(0, 1, 1)
        send(1, 2, -1)
        relay(0, 0, 1)

    @pl.when(v == 3)
    def _():
        send(1, 3, -2)
        send(1, 3, -1)
        arrive(0, 1)

    def relays(step):
        for at, where, b, p, way in RELAYS:
            @pl.when(jnp.logical_and(step == at, v == where))
            def _():
                relay_piece(1, b, p, way)

        @pl.when(jnp.logical_and(step == max(RELAYS)[0], v == 2))
        def _():
            send(1, 2, 1)

    def far_copy(u):
        return pltpu.make_async_remote_copy(
            src_ref=far_send.at[u], dst_ref=far_recv.at[u],
            send_sem=fs_sem.at[u], recv_sem=fr_sem.at[u],
            device_id={"narrow": mate}, device_id_type=MESH,
        )

    def near_copy(u):
        return pltpu.make_async_remote_copy(
            src_ref=near_send.at[u], dst_ref=near_recv.at[u],
            send_sem=ns_sem.at[u], recv_sem=nr_sem.at[u],
            device_id={"narrow": mate}, device_id_type=MESH,
        )

    def b_copy(u):
        return pltpu.make_async_remote_copy(
            src_ref=b_send.at[u], dst_ref=b_recv.at[u],
            send_sem=bs_sem.at[u], recv_sem=br_sem.at[u],
            device_id={"narrow": across}, device_id_type=MESH,
        )

    def cross(u):
        far_copy(u).wait_recv()
        for k in range(2):
            total = far_kept[u % kept_slots, k] + far_recv[u, k].astype(jnp.float32)
            b_send[u, k] = total.astype(jnp.bfloat16)
        b_copy(u).start()

    def tokens(model, *blocks):
        return jnp.concatenate([gath[model, i] for i in blocks], axis=0)

    def await_weights(u, model, j):
        for copy in weight_copies(u, model, j):
            copy.wait()

    def keep_far(u, k, out):
        far_kept[u % kept_slots, k] = out

    def give_far(u, k, out):
        far_send[u, k] = out.astype(jnp.bfloat16)

    def share_near(u, k, out):
        near_kept[u, k] = out[:rows]
        near_send[u, k] = out[rows:].astype(jnp.bfloat16)

    def refill(u):
        @pl.when(u + slots < units)
        def _():
            for copy in weight_copies(u + slots, 1, u + slots - per):
                copy.start()

    def phase(low, high, step0, body):
        def run(j, carry):
            relays(step0 + j - low)
            body(j)
            return carry
        lax.fori_loop(low, high, run, 0)
        return step0 + high - low

    def one_block(u, k, out, mine):
        @pl.when(mine)
        def _():
            keep_far(u, k, out)

        @pl.when(jnp.logical_not(mine))
        def _():
            give_far(u, k, out)

    def pass_on(u, mine):
        @pl.when(jnp.logical_not(mine))
        def _():
            far_copy(u).start()

        @pl.when(jnp.logical_and(mine, u >= LAG))
        def _():
            cross(u - LAG)

    def early(u):
        await_weights(u, 0, u)
        left = gath[0, first]
        for k in range(2):
            one_block(u, k, matmul(left, wbuf[u % slots, k]), leads)
        pass_on(u, leads)

    def rest(u):
        left = tokens(0, second, n, mate)
        for k in range(2):
            out = matmul(left, wbuf[u % slots, k])
            one_block(u, k, out[:rows], jnp.logical_not(leads))
            share_near(u, k, out[rows:])
        near_copy(u).start()
        pass_on(u, jnp.logical_not(leads))

        @pl.when(jnp.logical_and(leads, u < LAG))
        def _():
            cross(ahead[0] - LAG + u)

        refill(u)

    def whole(u, model):
        await_weights(u, model, u - model * per)
        left = tokens(model, across, beside, n, mate)
        for k in range(2):
            out = matmul(left, wbuf[u % slots, k])
            keep_far(u, k, out[:rows])
            give_far(u, k, out[rows:2 * rows])
            share_near(u, k, out[2 * rows:])
        far_copy(u).start()
        near_copy(u).start()

    def target(u):
        whole(u, 0)
        refill(u)

        @pl.when(jnp.logical_or(u >= ahead[0] + LAG, jnp.logical_not(leads)))
        def _():
            cross(u - LAG)

    def summed(u, k):
        near = near_kept[u, k] + near_recv[u, k].astype(jnp.float32)
        return near + b_recv[u, k].astype(jnp.float32)

    def activation(u):
        near_copy(u).wait_recv()
        b_copy(u).wait_recv()
        gate = summed(u, 0)
        return gate / (1.0 + jnp.exp(-gate)) * summed(u, 1)

    def finish_target(j):
        act = activation(j)
        kept[j] = act
        t_out[:, pl.ds(pl.multiple_of(j * tn, tn), tn)] = (live_ref[...] * act).astype(t_out.dtype)

    def finish_ratio(j, carry):
        act = activation(per + j)
        ratio = live_ref[...] * (kept[j] - weight_ref[...] * act)
        r_out[:, pl.ds(pl.multiple_of(j * tn, tn), tn)] = ratio.astype(r_out.dtype)
        return carry

    def source_far(j):
        u = per + j
        await_weights(u, 1, j)
        left = tokens(1, across, beside)
        for k in range(2):
            out = matmul(left, wbuf[u % slots, k])
            keep_far(u, k, out[:rows])
            give_far(u, k, out[rows:])
        far_copy(u).start()
        cross(u - LAG)

    def source_all(j):
        whole(per + j, 1)
        cross(per + j - LAG)
        finish_target(j - ahead[1])

    def source_near(j):
        u = per + j
        left = tokens(1, n, mate)
        for k in range(2):
            share_near(u, k, matmul(left, wbuf[u % slots, k]))
        near_copy(u).start()

        @pl.when(j < LAG)
        def _():
            cross(units - LAG + j)

        finish_target(per - ahead[1] + j)

    row = lax.broadcasted_iota(jnp.int32, (rows, 1), 0)
    hlen = rows // len_ref.shape[0]
    lived = jnp.zeros((rows, 1), jnp.float32)
    for h in range(len_ref.shape[0]):
        inside = jnp.logical_and(row >= h * hlen, row < h * hlen + len_ref[h])
        lived = jnp.where(inside, 1.0, lived)
    live_ref[...] = lived

    step = phase(0, ahead[0], 0, early)

    @pl.when(v == 0)
    def _():
        arrive(0, 1, 2, 3)

    @pl.when(v == 1)
    def _():
        arrive(0, 0)

    @pl.when(v == 2)
    def _():
        arrive(0, 3)

    @pl.when(v == 3)
    def _():
        arrive(0, 2, 0)

    step = phase(0, ahead[0], step, rest)
    step = phase(ahead[0], per, step, target)

    @pl.when(v == 0)
    def _():
        arrive(1, 1)

    @pl.when(v == 1)
    def _():
        arrive(1, 0)

    @pl.when(v == 3)
    def _():
        arrive(1, 1, 0)

    step = phase(0, ahead[1], step, source_far)

    @pl.when(v == 0)
    def _():
        arrive(1, 2, 3)

    @pl.when(v == 2)
    def _():
        arrive(1, 3)

    @pl.when(v == 3)
    def _():
        arrive(1, 2)

    step = phase(ahead[1], per, step, source_all)
    step = phase(0, ahead[1], step, source_near)

    fetch.wait()
    picked = jnp.zeros((rows, 1), jnp.float32)
    for i in range(rows):
        picked = jnp.where(row == i, table[ids_ref[i]], picked)
    weight_ref[...] = picked
    lax.fori_loop(0, per, finish_ratio, 0)

    def drain(u, carry):
        far_copy(u).wait_send()
        near_copy(u).wait_send()
        b_copy(u).wait_send()
        return carry

    lax.fori_loop(0, units, drain, 0)
    for m in range(2):
        for where, b, way in ((0, 0, 1), (0, 0, 2), (1, 1, 1), (1, 1, -1), (1, 2, -1), (1, 3, -1),
                              (2, 2, -1), (2, 2, 1), (2, 1, 1), (2, 0, 1), (3, 3, -1), (3, 3, -2)):
            @pl.when(v == where)
            def _():
                for p in range(PIECES[m]):
                    hop(m, b, p, way).wait_send()


def plan(states, weights, wide, narrow):
    depth, cols = weights.shape
    rows = states.shape[0]
    if narrow != 4 or wide != 4 or rows % 16 or depth % (128 * max(PIECES)):
        return None
    for tn in (512, 256):
        if cols % tn or cols // tn < 3:
            continue
        per = cols // tn
        ahead = [max(LAG, units * per // 7) for units in AHEAD]
        tile = rows * tn * 4
        fixed = 2 * wide * rows * depth * 2 + tile * (2 * per * (2 * 3 + 2) + 2 * (ahead[0] + LAG) + per)
        slots = (VMEM_BYTES - 1_500_000 - fixed) // (4 * tn * depth)
        slots = min(slots, 2 * per)
        if per - max(ahead) >= LAG and slots >= per + 2 and sum(ahead) + per > max(RELAYS)[0]:
            return tn, slots, ahead
    return None


def fused(states, weights, token_ids, lengths, ratio_weight, wide, tn, slots, ahead):
    rows, depth = states[0].shape
    cols = weights[0].shape[1]
    per = cols // tn
    units = 2 * per
    smem = pl.BlockSpec(memory_space=pltpu.SMEM)
    hbm = pl.BlockSpec(memory_space=pl.ANY)
    dma = pltpu.SemaphoreType.DMA
    wire = pltpu.VMEM((units, 2, rows, tn), jnp.bfloat16)
    held = pltpu.VMEM((rows, cols), jnp.bfloat16)
    vmem = pl.BlockSpec(memory_space=pltpu.VMEM)
    return pl.pallas_call(
        functools.partial(kernel, tn, slots, ahead),
        out_shape=(held, held),
        in_specs=[smem, smem] + [hbm] * 7,
        out_specs=(vmem, vmem),
        scratch_shapes=[
            pltpu.VMEM((2, wide, rows, depth), jnp.bfloat16),
            pltpu.VMEM((slots, 2, depth, tn), jnp.bfloat16),
            pltpu.VMEM((ahead[0] + LAG, 2, rows, tn), jnp.float32),
            pltpu.VMEM((units, 2, rows, tn), jnp.float32),
            wire, wire, wire, wire, wire, wire,
            pltpu.VMEM((per, rows, tn), jnp.float32),
            pltpu.VMEM((rows, 1), jnp.float32),
            pltpu.VMEM((rows, 1), jnp.float32),
            pltpu.SMEM(ratio_weight.shape, jnp.float32),
            dma,
            dma((2,)),
            dma((2, 3, wide, max(PIECES))),
            dma((2, wide, max(PIECES))),
            dma((slots, 2)),
            dma((units,)),
            dma((units,)),
            dma((units,)),
            dma((units,)),
            dma((units,)),
            dma((units,)),
        ],
        compiler_params=pltpu.CompilerParams(
            collective_id=0, has_side_effects=True, vmem_limit_bytes=VMEM_BYTES
        ),
        name="rescore",
    )(token_ids, lengths, ratio_weight, *states, *weights)


def local(
    wide,
    narrow,
    target_states,
    source_states,
    target_gate,
    target_up,
    source_gate,
    source_up,
    token_ids,
    lengths,
    ratio_weight,
):
    hidden_cols = target_gate.shape[1]
    own_rows = token_ids.shape[0]
    chosen = plan(target_states, target_gate, wide, narrow)
    if chosen is not None:
        return fused(
            (target_states, source_states),
            (target_gate, target_up, source_gate, source_up),
            token_ids,
            lengths,
            ratio_weight,
            wide,
            *chosen,
        )
    slot_count = own_rows // lengths.shape[0]
    slots = jnp.arange(slot_count, dtype=jnp.int32)
    live = (slots[None, :] < lengths[:, None]).reshape(-1).astype(jnp.float32)
    weight = ratio_weight[token_ids]
    target_terms = pair_project(
        target_gate, target_up, lax.all_gather(target_states, "wide", axis=0, tiled=True)
    )
    source_terms = pair_project(
        source_gate, source_up, lax.all_gather(source_states, "wide", axis=0, tiled=True)
    )
    target_sum, source_sum = (
        lax.psum_scatter(
            target_terms.astype(jnp.bfloat16), "narrow", scatter_dimension=0, tiled=True
        ).astype(jnp.float32),
        lax.psum_scatter(
            source_terms.astype(jnp.bfloat16), "narrow", scatter_dimension=0, tiled=True
        ).astype(jnp.float32),
    )
    target_act = gated(target_sum, hidden_cols)
    source_act = gated(source_sum, hidden_cols)
    target_out = (live[:, None] * target_act).astype(jnp.bfloat16)
    ratio_out = (live[:, None] * (target_act - weight[:, None] * source_act)).astype(jnp.bfloat16)
    return (target_out, ratio_out)


def solution(mesh):
    placed = (
        P(("groups", "wide"), "narrow"),
        P(("groups", "wide"), "narrow"),
        P("narrow", "wide"),
        P("narrow", "wide"),
        P("narrow", "wide"),
        P("narrow", "wide"),
        P(("groups", "narrow")),
        P(("groups", "narrow")),
        P(),
    )
    return jax.shard_map(
        functools.partial(local, mesh.shape["wide"], mesh.shape["narrow"]),
        mesh=mesh,
        in_specs=placed,
        out_specs=(P(("groups", "narrow"), "wide"), P(("groups", "narrow"), "wide")),
        check_vma=False,
    )
```
